32 devices in a mesh: dp: 2 (over x), ctx: 8 (over z, y), tp: 2 (over core).
Axes of the slice: x: 2, y: 2, z: 4, core: 2. Of those that a mesh axis runs over, the one named last changes fastest.
Arguments:
- inputs: bfloat16 [2, 4096, 1024], P('dp', 'tp', 'ctx'), may hold values from -6 to 6
- gate: bfloat16 [2, 4096, 1024], P('dp', 'tp', 'ctx'), may hold values from -6 to 6
- grad_out: bfloat16 [2, 4096, 1024], P('dp', 'tp', 'ctx'), may hold values from -0.125 to 0.125
- filters: float32 [4096, 1024], P('tp', 'ctx'), may hold values from -6 to 6
Outputs:
- grad_inputs: bfloat16 [2, 4096, 1024], P('dp', 'tp', 'ctx')
- grad_gate: bfloat16 [2, 4096, 1024], P('dp', 'tp', 'ctx')
- grad_filters: float32 [4096, 1024], P('tp', 'ctx')
The draws below stay inside these ranges and needn't reach their ends.
All inputs are finite; a program needn't handle non-finite values.
Results may differ from the reference program's by a relative error of at most 0.001.
Values may be sent and summed in bfloat16 or wider, within the bound.
A program may use at most 128 MiB of HBM per device.

```python
import jax
import jax.numpy as jnp
from jax import lax

CHANNELS = 4096
LENGTH = 1024
BATCH = 2


def level_of(own_key, shape, cuts, least, largest):
    factor_of, own = 1.0, jax.random.fold_in(own_key, 6)
    for dim, blocks in cuts:
        draws = jnp.exp(jax.random.uniform(jax.random.fold_in(own, dim), (blocks,), jnp.float32, least / len(cuts), largest / len(cuts)))
        factor_of = factor_of * jnp.repeat(draws, shape[dim] // blocks).reshape([-1 if axis == dim else 1 for axis in range(len(shape))])
    return factor_of


def noise(stream_key, dims, width, bound, cuts=(), kind=jnp.bfloat16):
    factor_of = level_of(stream_key, dims, cuts, -0.22, 0.18) if cuts else 1.0
    values = jax.random.normal(stream_key, dims, jnp.float32) * width * factor_of
    return jnp.minimum(jnp.maximum(values, -bound), bound).astype(kind)


def setup_inputs(seed: int = 0) -> dict:
    seeds = jax.random.split(jax.random.key(seed), 5)
    inputs = noise(seeds[0], (BATCH, CHANNELS, LENGTH), 1.0, 6.0, ((0, 2), (1, 2), (2, 8)))
    gate = noise(seeds[1], (BATCH, CHANNELS, LENGTH), 1.0, 6.0, ((0, 2), (1, 2), (2, 8)))
    grad_out = noise(seeds[2], (BATCH, CHANNELS, LENGTH), (1.0 / (2 * LENGTH) ** 0.5), 0.125, ((0, 2), (1, 2), (2, 8)))
    filters = noise(seeds[3], (CHANNELS, LENGTH), 1.0, 6.0, ((0, 2), (1, 8)), jnp.float32)
    return {"inputs": inputs, "gate": gate, "grad_out": grad_out, "filters": filters}


def reference(inputs, gate, grad_out, filters):
    seq_count, channels, length = inputs.shape
    block_width = min(512, channels)
    blocks = channels // block_width
    padded_len = 2 * length

    def regroup(array):
        return jnp.swapaxes(array.reshape(seq_count, blocks, block_width, length), 0, 1)

    def one_block(pieces):
        signal, gating, upstream, kernel = pieces
        signal = signal.astype(jnp.float32)
        upstream = upstream.astype(jnp.float32)
        product = upstream * gating.astype(jnp.float32)
        kernel_spec = jnp.fft.rfft(kernel.astype(jnp.float32), n=padded_len, axis=-1)
        signal_spec = jnp.fft.rfft(signal, n=padded_len, axis=-1)
        product_spec = jnp.fft.rfft(product, n=padded_len, axis=-1)
        response = jnp.fft.irfft(kernel_spec[None] * signal_spec, n=padded_len, axis=-1)[..., :length]
        back_signal = jnp.fft.irfft(jnp.conj(kernel_spec)[None] * product_spec, n=padded_len, axis=-1)[..., :length]
        lag_terms = jnp.fft.irfft(jnp.conj(signal_spec) * product_spec, n=padded_len, axis=-1)[..., :length]
        filter_grad = jnp.sum(lag_terms, axis=0).astype(jnp.float32)
        gate_grad = (upstream * response).astype(jnp.bfloat16)
        return back_signal.astype(jnp.bfloat16), gate_grad, filter_grad

    results = lax.map(one_block, (regroup(inputs), regroup(gate), regroup(grad_out), filters.reshape(blocks, block_width, length)))
    grad_inputs = jnp.swapaxes(results[0], 0, 1).reshape(seq_count, channels, length)
    grad_gate = jnp.swapaxes(results[1], 0, 1).reshape(seq_count, channels, length)
    grad_filters = results[2].reshape(channels, length)
    return (grad_inputs, grad_gate, grad_filters)
```

```python
import math
from functools import partial

import jax
import jax.numpy as jnp
import numpy as np
from jax import lax
from jax.experimental import pallas as pl
from jax.experimental.pallas import tpu as pltpu
from jax.sharding import PartitionSpec as P

BF16 = jnp.bfloat16
F32 = jnp.float32


def tables(groups, width):
    outer = 2 * groups
    total = outer * width
    freqs = groups + 1
    k1 = np.arange(freqs)[:, None, None]
    b = np.arange(width)[None, :, None]
    k2 = np.arange(width)[None, None, :]
    angle = 2.0 * math.pi * ((b * (k1 + outer * k2)) % total) / total
    cosine, sine = np.cos(angle), -np.sin(angle)
    top = np.concatenate([cosine, sine], axis=2)
    bottom = np.concatenate([-sine, cosine], axis=2)
    matrix = np.concatenate([top, bottom], axis=1).astype(np.float32)
    high = matrix.astype(BF16)
    low = (matrix - high.astype(np.float32)).astype(BF16)
    phase = 2.0 * math.pi * ((np.arange(freqs)[:, None] * np.arange(groups)[None, :]) % outer) / outer
    weight = np.full((freqs, 1), 2.0)
    weight[0] = weight[-1] = 1.0
    weight = weight / total
    coef = np.stack([np.cos(phase), -np.sin(phase), weight * np.cos(phase), -weight * np.sin(phase)], axis=1)
    return high, low, coef.reshape(freqs * 4, groups).astype(np.float32)


def split(value):
    high = value.astype(BF16)
    return high, (value - high.astype(F32)).astype(BF16)


def transform_kernel(coef, x_ref, dy_ref, gate_ref, f_ref, mh_ref, ml_ref, gi_ref, gg_ref, gf_ref, sig, a_hi, a_lo, spec, acc):
    groups, owned, width = x_ref.shape
    step = pl.program_id(0)
    rows = min(32, owned)
    chunks = owned // rows

    @pl.when(step == 0)
    def _():
        def fill(r, _):
            at = pl.ds(pl.multiple_of(r * rows, rows), rows)
            for a in range(groups):
                sig[0, a, at, :] = x_ref[a, at, :].astype(F32)
                sig[1, a, at, :] = dy_ref[a, at, :].astype(F32) * gate_ref[a, at, :].astype(F32)
                sig[2, a, at, :] = f_ref[a, at, :]
                for s in range(3):
                    acc[s, a, at, :] = jnp.zeros((rows, width), F32)
            return 0

        lax.fori_loop(0, chunks, fill, 0)

    base = step * 4

    def forward(r, _):
        at = pl.ds(pl.multiple_of(r * rows, rows), rows)
        for s in range(3):
            real = imag = None
            for a in range(groups):
                value = sig[s, a, at, :]
                re, im = value * coef[base, a], value * coef[base + 1, a]
                real = re if real is None else real + re
                imag = im if imag is None else imag + im
            a_hi[s, at, :width], a_lo[s, at, :width] = split(real)
            a_hi[s, at, width:], a_lo[s, at, width:] = split(imag)
        return 0

    lax.fori_loop(0, chunks, forward, 0)

    def multiply(contract):
        dims = (((1,), (contract,)), ((), ()))
        dot = partial(lax.dot_general, dimension_numbers=dims, preferred_element_type=F32)
        for s in range(3):
            high, low = a_hi[s], a_lo[s]
            spec[s] = dot(high, mh_ref[0]) + dot(low, mh_ref[0]) + dot(high, ml_ref[0])

    multiply(0)

    def pointwise(r, _):
        at = pl.ds(pl.multiple_of(r * rows, rows), rows)
        xr, xi = spec[0, at, :width], spec[0, at, width:]
        pr, pi = spec[1, at, :width], spec[1, at, width:]
        fr, fi = spec[2, at, :width], spec[2, at, width:]
        terms = (
            (fr * xr - fi * xi, fr * xi + fi * xr),
            (fr * pr + fi * pi, fr * pi - fi * pr),
            (xr * pr + xi * pi, xr * pi - xi * pr),
        )
        for s, (real, imag) in enumerate(terms):
            a_hi[s, at, :width], a_lo[s, at, :width] = split(real)
            a_hi[s, at, width:], a_lo[s, at, width:] = split(imag)
        return 0

    lax.fori_loop(0, chunks, pointwise, 0)
    multiply(1)

    def inverse(r, _):
        at = pl.ds(pl.multiple_of(r * rows, rows), rows)
        for s in range(3):
            real, imag = spec[s, at, :width], spec[s, at, width:]
            for a in range(groups):
                acc[s, a, at, :] += real * coef[base + 2, a] + imag * coef[base + 3, a]
        return 0

    lax.fori_loop(0, chunks, inverse, 0)

    @pl.when(step == pl.num_programs(0) - 1)
    def _():
        def finish(r, _):
            at = pl.ds(pl.multiple_of(r * rows, rows), rows)
            for a in range(groups):
                gg_ref[a, at, :] = (dy_ref[a, at, :].astype(F32) * acc[0, a, at, :]).astype(BF16)
                gi_ref[a, at, :] = acc[1, a, at, :].astype(BF16)
                gf_ref[a, at, :] = acc[2, a, at, :]
            return 0

        lax.fori_loop(0, chunks, finish, 0)


def transform(x, dy, gate, filters, interpret=False):
    groups, owned, width = x.shape
    high, low, coef = tables(groups, width)
    freqs = groups + 1
    whole = pl.BlockSpec((groups, owned, width), lambda k: (0, 0, 0))
    table = pl.BlockSpec((1, 2 * width, 2 * width), lambda k: (k, 0, 0))
    shape = (groups, owned, width)
    return pl.pallas_call(
        transform_kernel,
        grid=(freqs,),
        in_specs=[pl.BlockSpec(memory_space=pltpu.SMEM), whole, whole, whole, whole, table, table],
        out_specs=[whole, whole, whole],
        out_shape=[
            jax.ShapeDtypeStruct(shape, BF16),
            jax.ShapeDtypeStruct(shape, BF16),
            jax.ShapeDtypeStruct(shape, F32),
        ],
        scratch_shapes=[
            pltpu.VMEM((3, groups, owned, width), F32),
            pltpu.VMEM((3, owned, 2 * width), BF16),
            pltpu.VMEM((3, owned, 2 * width), BF16),
            pltpu.VMEM((3, owned, 2 * width), F32),
            pltpu.VMEM((3, groups, owned, width), F32),
        ],
        compiler_params=pltpu.CompilerParams(vmem_limit_bytes=48 * 1024 * 1024),
        interpret=interpret,
    )(coef, x, dy, gate, filters, high, low)


def shards(inputs, gate, grad_out, filters):
    groups = lax.axis_size("ctx")
    channels, width = inputs.shape[1:]
    owned = channels // groups
    swap = partial(lax.all_to_all, axis_name="ctx", split_axis=0, concat_axis=0, tiled=True)

    def blocks(array):
        return array.reshape(groups, owned, width)

    x, dy, g, f = (swap(blocks(v)) for v in (inputs, grad_out, gate, filters))
    gi, gg, gf = transform(x, dy, g, f)
    gf = swap(lax.psum(gf, "dp"))
    return (
        swap(gi).reshape(1, channels, width),
        swap(gg).reshape(1, channels, width),
        gf.reshape(channels, width),
    )


def solution(mesh):
    placed = (P("dp", "tp", "ctx"), P("dp", "tp", "ctx"), P("dp", "tp", "ctx"), P("tp", "ctx"))
    return jax.shard_map(
        shards,
        mesh=mesh,
        in_specs=placed,
        out_specs=(P("dp", "tp", "ctx"), P("dp", "tp", "ctx"), P("tp", "ctx")),
        check_vma=False,
    )
```

```python
import math
from functools import partial

import jax
import jax.numpy as jnp
import numpy as np
from jax import lax
from jax.experimental import pallas as pl
from jax.experimental.pallas import tpu as pltpu
from jax.sharding import PartitionSpec as P

BF16 = jnp.bfloat16
F32 = jnp.float32
MESH = pl.DeviceIdType.MESH


def tables(groups, width):
    outer = 2 * groups
    total = outer * width
    freqs = groups + 1
    k1 = np.arange(freqs)[:, None, None]
    b = np.arange(width)[None, :, None]
    k2 = np.arange(width)[None, None, :]
    angle = 2.0 * math.pi * ((b * (k1 + outer * k2)) % total) / total
    cosine, sine = np.cos(angle), -np.sin(angle)
    top = np.concatenate([cosine, sine], axis=2)
    bottom = np.concatenate([-sine, cosine], axis=2)
    matrix = np.concatenate([top, bottom], axis=1).astype(np.float32)
    high = matrix.astype(BF16)
    low = (matrix - high.astype(np.float32)).astype(BF16)
    phase = 2.0 * math.pi * ((np.arange(freqs)[:, None] * np.arange(groups)[None, :]) % outer) / outer
    weight = np.full((freqs, 1), 2.0)
    weight[0] = weight[-1] = 1.0
    weight = weight / total
    coef = np.stack([np.cos(phase), -np.sin(phase), weight * np.cos(phase), -weight * np.sin(phase)], axis=1)
    return high, low, coef.reshape(freqs * 4, groups).astype(np.float32)


def split(value):
    high = value.astype(BF16)
    return high, (value - high.astype(F32)).astype(BF16)


def transform_kernel(coef, x_ref, dy_ref, gate_ref, f_ref, mh_ref, ml_ref, gi_ref, gg_ref, gf_ref, sig, a_hi, a_lo, spec, acc):
    groups, owned, width = x_ref.shape
    step = pl.program_id(0)
    rows = min(32, owned)
    chunks = owned // rows

    @pl.when(step == 0)
    def _():
        def fill(r, _):
            at = pl.ds(pl.multiple_of(r * rows, rows), rows)
            for a in range(groups):
                sig[0, a, at, :] = x_ref[a, at, :].astype(F32)
                sig[1, a, at, :] = dy_ref[a, at, :].astype(F32) * gate_ref[a, at, :].astype(F32)
                sig[2, a, at, :] = f_ref[a, at, :]
                for s in range(3):
                    acc[s, a, at, :] = jnp.zeros((rows, width), F32)
            return 0

        lax.fori_loop(0, chunks, fill, 0)

    base = step * 4

    def forward(r, _):
        at = pl.ds(pl.multiple_of(r * rows, rows), rows)
        for s in range(3):
            real = imag = None
            for a in range(groups):
                value = sig[s, a, at, :]
                re, im = value * coef[base, a], value * coef[base + 1, a]
                real = re if real is None else real + re
                imag = im if imag is None else imag + im
            a_hi[s, at, :width], a_lo[s, at, :width] = split(real)
            a_hi[s, at, width:], a_lo[s, at, width:] = split(imag)
        return 0

    lax.fori_loop(0, chunks, forward, 0)

    def multiply(contract):
        dims = (((1,), (contract,)), ((), ()))
        dot = partial(lax.dot_general, dimension_numbers=dims, preferred_element_type=F32)
        for s in range(3):
            high, low = a_hi[s], a_lo[s]
            spec[s] = dot(high, mh_ref[0]) + dot(low, mh_ref[0]) + dot(high, ml_ref[0])

    multiply(0)

    def pointwise(r, _):
        at = pl.ds(pl.multiple_of(r * rows, rows), rows)
        xr, xi = spec[0, at, :width], spec[0, at, width:]
        pr, pi = spec[1, at, :width], spec[1, at, width:]
        fr, fi = spec[2, at, :width], spec[2, at, width:]
        terms = (
            (fr * xr - fi * xi, fr * xi + fi * xr),
            (fr * pr + fi * pi, fr * pi - fi * pr),
            (xr * pr + xi * pi, xr * pi - xi * pr),
        )
        for s, (real, imag) in enumerate(terms):
            a_hi[s, at, :width], a_lo[s, at, :width] = split(real)
            a_hi[s, at, width:], a_lo[s, at, width:] = split(imag)
        return 0

    lax.fori_loop(0, chunks, pointwise, 0)
    multiply(1)

    def inverse(r, _):
        at = pl.ds(pl.multiple_of(r * rows, rows), rows)
        for s in range(3):
            real, imag = spec[s, at, :width], spec[s, at, width:]
            for a in range(groups):
                acc[s, a, at, :] += real * coef[base + 2, a] + imag * coef[base + 3, a]
        return 0

    lax.fori_loop(0, chunks, inverse, 0)

    @pl.when(step == pl.num_programs(0) - 1)
    def _():
        def finish(r, _):
            at = pl.ds(pl.multiple_of(r * rows, rows), rows)
            for a in range(groups):
                gg_ref[a, at, :] = (dy_ref[a, at, :].astype(F32) * acc[0, a, at, :]).astype(BF16)
                gi_ref[a, at, :] = acc[1, a, at, :].astype(BF16)
                gf_ref[a, at, :] = acc[2, a, at, :]
            return 0

        lax.fori_loop(0, chunks, finish, 0)


def transform(x, dy, gate, filters, interpret=False):
    groups, owned, width = x.shape
    high, low, coef = tables(groups, width)
    freqs = groups + 1
    whole = pl.BlockSpec((groups, owned, width), lambda k: (0, 0, 0))
    table = pl.BlockSpec((1, 2 * width, 2 * width), lambda k: (k, 0, 0))
    shape = (groups, owned, width)
    return pl.pallas_call(
        transform_kernel,
        grid=(freqs,),
        in_specs=[pl.BlockSpec(memory_space=pltpu.SMEM), whole, whole, whole, whole, table, table],
        out_specs=[whole, whole, whole],
        out_shape=[
            jax.ShapeDtypeStruct(shape, BF16),
            jax.ShapeDtypeStruct(shape, BF16),
            jax.ShapeDtypeStruct(shape, F32),
        ],
        scratch_shapes=[
            pltpu.VMEM((3, groups, owned, width), F32),
            pltpu.VMEM((3, owned, 2 * width), BF16),
            pltpu.VMEM((3, owned, 2 * width), BF16),
            pltpu.VMEM((3, owned, 2 * width), F32),
            pltpu.VMEM((3, groups, owned, width), F32),
        ],
        compiler_params=pltpu.CompilerParams(vmem_limit_bytes=48 * 1024 * 1024),
        interpret=interpret,
    )(coef, x, dy, gate, filters, high, low)


def greet(me, groups, twin):
    barrier = pltpu.get_barrier_semaphore()

    def hail(o, _):
        pl.semaphore_signal(barrier, inc=1, device_id={"ctx": lax.rem(me + o, groups)}, device_id_type=MESH)
        return 0

    lax.fori_loop(1, groups, hail, 0)
    pl.semaphore_signal(barrier, inc=1, device_id={"dp": twin}, device_id_type=MESH)
    pl.semaphore_wait(barrier, groups)


def gather_kernel(groups, *refs):
    sources, targets = refs[:4], refs[4:8]
    send, recv, pass_send, pass_recv, local = refs[8:]
    owned = sources[0].shape[1]
    half = owned // 2
    me, dp = lax.axis_index("ctx"), lax.axis_index("dp")
    twin = 1 - dp
    mine = pl.ds(pl.multiple_of(dp * half, half), half)
    theirs = pl.ds(pl.multiple_of(twin * half, half), half)

    def push(s, peer, slot, sem):
        source, target = sources[s].at[peer], targets[s].at[slot]
        if s == 0:
            source, target = sources[0].at[peer, mine], targets[0].at[slot, mine]
        return pltpu.make_async_remote_copy(
            src_ref=source,
            dst_ref=target,
            send_sem=send.at[s, peer],
            recv_sem=recv.at[s, sem],
            device_id={"ctx": peer},
            device_id_type=MESH,
        )

    def hand(slot, rows):
        return pltpu.make_async_remote_copy(
            src_ref=targets[0].at[slot, rows],
            dst_ref=targets[0].at[slot, rows],
            send_sem=pass_send.at[slot],
            recv_sem=pass_recv.at[slot],
            device_id={"dp": twin},
            device_id_type=MESH,
        )

    def keep(s):
        return pltpu.make_async_copy(sources[s].at[me], targets[s].at[me], local.at[s])

    greet(me, groups, twin)
    for s in range(4):

        def start(o, _):
            push(s, lax.rem(me + o, groups), me, me).start()
            return 0

        lax.fori_loop(1, groups, start, 0)
        keep(s).start()

    def relay(o, _):
        origin = lax.rem(me + groups - o, groups)
        push(0, origin, origin, origin).wait_recv()
        hand(origin, mine).start()
        return 0

    lax.fori_loop(1, groups, relay, 0)
    for s in range(4):

        def finish(o, _):
            origin = lax.rem(me + groups - o, groups)
            if s:
                push(s, origin, origin, origin).wait_recv()
            else:
                hand(origin, mine).wait_send()
                hand(origin, theirs).wait_recv()
            push(s, origin, origin, origin).wait_send()
            return 0

        lax.fori_loop(1, groups, finish, 0)
        keep(s).wait()


def gather(filters, *signals):
    groups = filters.shape[0]
    arrays = (filters,) + signals
    anywhere = pl.BlockSpec(memory_space=pl.ANY)
    dma = pltpu.SemaphoreType.DMA
    return pl.pallas_call(
        partial(gather_kernel, groups),
        in_specs=[anywhere] * 4,
        out_specs=[anywhere] * 4,
        out_shape=[jax.ShapeDtypeStruct(v.shape, v.dtype) for v in arrays],
        scratch_shapes=[dma((4, groups)), dma((4, groups)), dma((groups,)), dma((groups,)), dma((4,))],
        compiler_params=pltpu.CompilerParams(collective_id=0, has_side_effects=True),
    )(*arrays)


def scatter_kernel(groups, gf_ref, gi_ref, gg_ref, ogf_ref, ogi_ref, ogg_ref, inbox, total, *sems):
    send, recv, twin_send, twin_recv, pass_send, pass_recv, local = sems
    owned = gf_ref.shape[1]
    half = owned // 2
    me, dp = lax.axis_index("ctx"), lax.axis_index("dp")
    twin = 1 - dp
    mine = pl.ds(pl.multiple_of(dp * half, half), half)
    theirs = pl.ds(pl.multiple_of(twin * half, half), half)
    sources, targets = (total, gi_ref, gg_ref), (ogf_ref, ogi_ref, ogg_ref)

    def push(s, peer, slot):
        target = targets[s].at[slot]
        if s == 0:
            target = ogf_ref.at[slot, mine]
        return pltpu.make_async_remote_copy(
            src_ref=sources[s].at[peer],
            dst_ref=target,
            send_sem=send.at[s, peer],
            recv_sem=recv.at[s, slot],
            device_id={"ctx": peer},
            device_id_type=MESH,
        )

    def trade(a):
        return pltpu.make_async_remote_copy(
            src_ref=gf_ref.at[a, theirs],
            dst_ref=inbox.at[a],
            send_sem=twin_send.at[a],
            recv_sem=twin_recv.at[a],
            device_id={"dp": twin},
            device_id_type=MESH,
        )

    def hand(source, slot, rows):
        return pltpu.make_async_remote_copy(
            src_ref=source,
            dst_ref=ogf_ref.at[slot, rows],
            send_sem=pass_send.at[slot],
            recv_sem=pass_recv.at[slot],
            device_id={"dp": twin},
            device_id_type=MESH,
        )

    def keep(s):
        target = ogf_ref.at[me, mine] if s == 0 else targets[s].at[me]
        return pltpu.make_async_copy(sources[s].at[me], target, local.at[s])

    greet(me, groups, twin)

    def open_trade(o, _):
        trade(lax.rem(me + o, groups)).start()
        return 0

    lax.fori_loop(1, groups + 1, open_trade, 0)
    for s in (1, 2):

        def start(o, _):
            push(s, lax.rem(me + o, groups), me).start()
            return 0

        lax.fori_loop(1, groups, start, 0)
        keep(s).start()

    def add(a):
        trade(a).wait_recv()
        total[a] = gf_ref[a, mine, :] + inbox[a]

    def reduce(o, _):
        peer = lax.rem(me + o, groups)
        add(peer)
        push(0, peer, me).start()
        return 0

    lax.fori_loop(1, groups, reduce, 0)
    add(me)
    keep(0).start()
    hand(total.at[me], me, mine).start()

    def relay(o, _):
        origin = lax.rem(me + groups - o, groups)
        push(0, origin, origin).wait_recv()
        hand(ogf_ref.at[origin, mine], origin, mine).start()
        return 0

    lax.fori_loop(1, groups, relay, 0)

    def settle(a, _):
        trade(a).wait_send()
        hand(total.at[me], a, mine).wait_send()
        hand(total.at[me], a, theirs).wait_recv()
        return 0

    lax.fori_loop(0, groups, settle, 0)
    for s in range(3):

        def finish(o, _):
            origin = lax.rem(me + groups - o, groups)
            if s:
                push(s, origin, origin).wait_recv()
            push(s, origin, origin).wait_send()
            return 0

        lax.fori_loop(1, groups, finish, 0)
        keep(s).wait()


def scatter(gf, gi, gg):
    groups, owned, width = gf.shape
    arrays = (gf, gi, gg)
    anywhere = pl.BlockSpec(memory_space=pl.ANY)
    vmem = pl.BlockSpec(memory_space=pltpu.VMEM)
    dma = pltpu.SemaphoreType.DMA
    return pl.pallas_call(
        partial(scatter_kernel, groups),
        in_specs=[vmem, anywhere, anywhere],
        out_specs=[anywhere] * 3,
        out_shape=[jax.ShapeDtypeStruct(v.shape, v.dtype) for v in arrays],
        scratch_shapes=[pltpu.VMEM((groups, owned // 2, width), F32)] * 2
        + [dma((3, groups)), dma((3, groups))]
        + [dma((groups,))] * 4
        + [dma((3,))],
        compiler_params=pltpu.CompilerParams(collective_id=1, has_side_effects=True),
    )(*arrays)


def shards(inputs, gate, grad_out, filters):
    groups = lax.axis_size("ctx")
    channels, width = inputs.shape[1:]
    owned = channels // groups
    def blocks(array):
        return array.reshape(groups, owned, width)

    f, x, dy, g = gather(*(blocks(v) for v in (filters, inputs, grad_out, gate)))
    gi, gg, gf = transform(x, dy, g, f)
    gf, gi, gg = scatter(gf, gi, gg)
    return (
        gi.reshape(1, channels, width),
        gg.reshape(1, channels, width),
        gf.reshape(channels, width),
    )


def solution(mesh):
    placed = (P("dp", "tp", "ctx"), P("dp", "tp", "ctx"), P("dp", "tp", "ctx"), P("tp", "ctx"))
    return jax.shard_map(
        shards,
        mesh=mesh,
        in_specs=placed,
        out_specs=(P("dp", "tp", "ctx"), P("dp", "tp", "ctx"), P("tp", "ctx")),
        check_vma=False,
    )
```

```python
import math
from functools import partial

import jax
import jax.numpy as jnp
import numpy as np
from jax import lax
from jax.experimental import pallas as pl
from jax.experimental.pallas import tpu as pltpu
from jax.sharding import PartitionSpec as P

BF16 = jnp.bfloat16
F32 = jnp.float32
PARTS = 2
MESH = pl.DeviceIdType.MESH


def tables(groups, width):
    outer = 2 * groups
    total = outer * width
    freqs = groups + 1
    k1 = np.arange(freqs)[:, None, None]
    b = np.arange(width)[None, :, None]
    k2 = np.arange(width)[None, None, :]
    angle = 2.0 * math.pi * ((b * (k1 + outer * k2)) % total) / total
    cosine, sine = np.cos(angle), -np.sin(angle)
    top = np.concatenate([cosine, sine], axis=2)
    bottom = np.concatenate([-sine, cosine], axis=2)
    matrix = np.concatenate([top, bottom], axis=1).astype(np.float32)
    high = matrix.astype(BF16)
    low = (matrix - high.astype(np.float32)).astype(BF16)
    phase = 2.0 * math.pi * ((np.arange(freqs)[:, None] * np.arange(groups)[None, :]) % outer) / outer
    weight = np.full((freqs, 1), 2.0)
    weight[0] = weight[-1] = 1.0
    weight = weight / total
    coef = np.stack([np.cos(phase), -np.sin(phase), weight * np.cos(phase), -weight * np.sin(phase)], axis=1)
    return high, low, coef.reshape(freqs * 4, groups).astype(np.float32)


def split(value):
    high = value.astype(BF16)
    return high, (value - high.astype(F32)).astype(BF16)


def greet(me, groups, twin):
    barrier = pltpu.get_barrier_semaphore()

    def hail(o, _):
        pl.semaphore_signal(barrier, inc=1, device_id={"ctx": lax.rem(me + o, groups)}, device_id_type=MESH)
        return 0

    lax.fori_loop(1, groups, hail, 0)
    pl.semaphore_signal(barrier, inc=1, device_id={"dp": twin}, device_id_type=MESH)
    pl.semaphore_wait(barrier, groups)


def fused_kernel(groups, parts, coef, mh_ref, ml_ref, f_ref, x_ref, dy_ref, gate_ref, ogf_ref, ogi_ref, ogg_ref, *scratch):
    (filt, recv_sig, sig, a_hi, a_lo, spec, acc, gf, gi, gg, inbox, total) = scratch[:12]
    (f_send, f_recv, f_pass_send, f_pass_recv, x_send, x_recv, keep_sem) = scratch[12:19]
    (o_send, o_recv, twin_send, twin_recv, pass_send, pass_recv, out_sem) = scratch[19:]
    owned, width = f_ref.shape[1:]
    chunk = owned // parts
    half, slim = owned // 2, chunk // 2
    rows = min(32, chunk)
    pieces = chunk // rows
    me, dp = lax.axis_index("ctx"), lax.axis_index("dp")
    twin = 1 - dp
    sources = (x_ref, dy_ref, gate_ref)

    def f_rows(which):
        return pl.ds(pl.multiple_of(which * half, half), half)

    def part(q):
        return pl.ds(q * chunk, chunk)

    def slim_rows(q, which):
        return pl.ds(pl.multiple_of(q * chunk + which * slim, slim), slim)

    def remote(source, target, send, recv, device):
        return pltpu.make_async_remote_copy(
            src_ref=source, dst_ref=target, send_sem=send, recv_sem=recv, device_id=device, device_id_type=MESH
        )

    def f_push(peer, slot):
        return remote(
            f_ref.at[peer, f_rows(dp)], filt.at[slot, f_rows(dp)], f_send.at[peer], f_recv.at[slot], {"ctx": peer}
        )

    def f_hand(slot, which):
        block = filt.at[slot, f_rows(which)]
        return remote(block, block, f_pass_send.at[slot], f_pass_recv.at[slot], {"dp": twin})

    def x_push(s, q, peer, slot):
        return remote(
            sources[s].at[peer, part(q)],
            recv_sig.at[s, slot, part(q)],
            x_send.at[s, q, peer],
            x_recv.at[s, q, slot],
            {"ctx": peer},
        )

    def keep(s):
        if s == 3:
            return pltpu.make_async_copy(f_ref.at[me], filt.at[me], keep_sem.at[3])
        return pltpu.make_async_copy(sources[s].at[me], recv_sig.at[s, me], keep_sem.at[s])

    def trade(q, a):
        return remote(
            gf.at[a, slim_rows(q, twin)], inbox.at[q, a], twin_send.at[q, a], twin_recv.at[q, a], {"dp": twin}
        )

    def out_push(s, q, peer, slot):
        if s == 0:
            source, target = total.at[q, peer], ogf_ref.at[slot, slim_rows(q, dp)]
        else:
            source, target = (gi, gg)[s - 1].at[peer, part(q)], (ogi_ref, ogg_ref)[s - 1].at[slot, part(q)]
        return remote(source, target, o_send.at[s, q, peer], o_recv.at[s, q, slot], {"ctx": peer})

    def out_keep(s, q):
        if s == 0:
            return pltpu.make_async_copy(total.at[q, me], ogf_ref.at[me, slim_rows(q, dp)], out_sem.at[0, q])
        source, target = (gi, gg)[s - 1].at[me, part(q)], (ogi_ref, ogg_ref)[s - 1].at[me, part(q)]
        return pltpu.make_async_copy(source, target, out_sem.at[s, q])

    def hand(source, q, slot, which):
        return remote(
            source, ogf_ref.at[slot, slim_rows(q, which)], pass_send.at[q, slot], pass_recv.at[q, slot], {"dp": twin}
        )

    def each(first, body, last=groups):
        def run(o, _):
            body(lax.rem(me + o, groups), lax.rem(me + groups - o, groups))
            return 0

        lax.fori_loop(first, last, run, 0)

    def compute(q):
        def by_rows(body):
            def run(r, _):
                body(pl.multiple_of(r * rows, rows))
                return 0

            lax.fori_loop(0, pieces, run, 0)

        def fill(at):
            near, far = pl.ds(at, rows), pl.ds(pl.multiple_of(at + q * chunk, rows), rows)
            for a in range(groups):
                sig[0, a, near, :] = recv_sig[0, a, far, :].astype(F32)
                sig[1, a, near, :] = recv_sig[1, a, far, :].astype(F32) * recv_sig[2, a, far, :].astype(F32)
                sig[2, a, near, :] = filt[a, far, :]
                for s in range(3):
                    acc[s, a, near, :] = jnp.zeros((rows, width), F32)

        by_rows(fill)

        def frequency(k, _):
            base = k * 4

            def put(s, at, real, imag):
                to = pl.ds(pl.multiple_of(at + s * chunk, rows), rows)
                a_hi[to, :width], a_lo[to, :width] = split(real)
                a_hi[to, width:], a_lo[to, width:] = split(imag)

            def take(s, at):
                to = pl.ds(pl.multiple_of(at + s * chunk, rows), rows)
                return spec[to, :width], spec[to, width:]

            def forward(at):
                for s in range(3):
                    real = imag = None
                    for a in range(groups):
                        value = sig[s, a, pl.ds(at, rows), :]
                        re, im = value * coef[base, a], value * coef[base + 1, a]
                        real = re if real is None else real + re
                        imag = im if imag is None else imag + im
                    put(s, at, real, imag)

            def multiply(contract):
                dims = (((1,), (contract,)), ((), ()))
                dot = partial(lax.dot_general, dimension_numbers=dims, preferred_element_type=F32)
                high, low = a_hi[...], a_lo[...]
                spec[...] = dot(high, mh_ref[k]) + dot(low, mh_ref[k]) + dot(high, ml_ref[k])

            def pointwise(at):
                (xr, xi), (pr, pi), (fr, fi) = take(0, at), take(1, at), take(2, at)
                put(0, at, fr * xr - fi * xi, fr * xi + fi * xr)
                put(1, at, fr * pr + fi * pi, fr * pi - fi * pr)
                put(2, at, xr * pr + xi * pi, xr * pi - xi * pr)

            def inverse(at):
                for s in range(3):
                    real, imag = take(s, at)
                    for a in range(groups):
                        acc[s, a, pl.ds(at, rows), :] += real * coef[base + 2, a] + imag * coef[base + 3, a]

            by_rows(forward)
            multiply(0)
            by_rows(pointwise)
            multiply(1)
            by_rows(inverse)
            return 0

        lax.fori_loop(0, groups + 1, frequency, 0)

        def finish(at):
            near, far = pl.ds(at, rows), pl.ds(pl.multiple_of(at + q * chunk, rows), rows)
            for a in range(groups):
                gg[a, far, :] = (recv_sig[1, a, far, :].astype(F32) * acc[0, a, near, :]).astype(BF16)
                gi[a, far, :] = acc[1, a, near, :].astype(BF16)
                gf[a, far, :] = acc[2, a, near, :]

        by_rows(finish)

    greet(me, groups, twin)
    each(1, lambda to, origin: f_push(to, me).start())
    for q in range(parts):
        for s in range(3):
            each(1, lambda to, origin, s=s, q=q: x_push(s, q, to, me).start())
    for s in range(4):
        keep(s).start()

    def f_relay(to, origin):
        f_push(origin, origin).wait_recv()
        f_hand(origin, dp).start()

    each(1, f_relay)

    def f_settle(to, origin):
        f_hand(origin, dp).wait_send()
        f_hand(origin, twin).wait_recv()
        f_push(origin, origin).wait_send()

    each(1, f_settle)
    for s in range(4):
        keep(s).wait()
    for q in range(parts):
        for s in range(3):
            each(1, lambda to, origin, s=s, q=q: x_push(s, q, origin, origin).wait_recv())
        compute(q)
        each(1, lambda to, origin, q=q: trade(q, to).start(), groups + 1)
        for s in (1, 2):
            each(1, lambda to, origin, s=s, q=q: out_push(s, q, to, me).start())
            out_keep(s, q).start()

    for q in range(parts):

        def add(a, q=q):
            trade(q, a).wait_recv()
            total[q, a] = gf[a, slim_rows(q, dp), :] + inbox[q, a]

        def reduce(to, origin, q=q, add=add):
            add(to)
            out_push(0, q, to, me).start()

        each(1, reduce)
        add(me)
        out_keep(0, q).start()
        hand(total.at[q, me], q, me, dp).start()
    for q in range(parts):

        def relay(to, origin, q=q):
            out_push(0, q, origin, origin).wait_recv()
            hand(ogf_ref.at[origin, slim_rows(q, dp)], q, origin, dp).start()

        each(1, relay)
    for q in range(parts):

        def settle(a, origin, q=q):
            trade(q, a).wait_send()
            hand(total.at[q, me], q, a, dp).wait_send()
            hand(total.at[q, me], q, a, twin).wait_recv()

        each(1, settle, groups + 1)
        for s in range(3):

            def done(to, origin, q=q, s=s):
                x_push(s, q, origin, origin).wait_send()
                if s:
                    out_push(s, q, origin, origin).wait_recv()
                out_push(s, q, origin, origin).wait_send()

            each(1, done)
            out_keep(s, q).wait()


def fused(f, x, dy, gate):
    groups, owned, width = f.shape
    parts = PARTS if owned % (16 * PARTS) == 0 else 1
    chunk = owned // parts
    high, low, coef = tables(groups, width)
    anywhere = pl.BlockSpec(memory_space=pl.ANY)
    vmem = pl.BlockSpec(memory_space=pltpu.VMEM)
    dma = pltpu.SemaphoreType.DMA
    shape = (groups, owned, width)
    slim = (parts, groups, chunk // 2, width)
    return pl.pallas_call(
        partial(fused_kernel, groups, parts),
        in_specs=[pl.BlockSpec(memory_space=pltpu.SMEM), vmem, vmem] + [anywhere] * 4,
        out_specs=[anywhere] * 3,
        out_shape=[
            jax.ShapeDtypeStruct(shape, F32),
            jax.ShapeDtypeStruct(shape, BF16),
            jax.ShapeDtypeStruct(shape, BF16),
        ],
        scratch_shapes=[
            pltpu.VMEM(shape, F32),
            pltpu.VMEM((3,) + shape, BF16),
            pltpu.VMEM((3, groups, chunk, width), F32),
            pltpu.VMEM((3 * chunk, 2 * width), BF16),
            pltpu.VMEM((3 * chunk, 2 * width), BF16),
            pltpu.VMEM((3 * chunk, 2 * width), F32),
            pltpu.VMEM((3, groups, chunk, width), F32),
            pltpu.VMEM(shape, F32),
            pltpu.VMEM(shape, BF16),
            pltpu.VMEM(shape, BF16),
            pltpu.VMEM(slim, F32),
            pltpu.VMEM(slim, F32),
        ]
        + [dma((groups,))] * 4
        + [dma((3, parts, groups))] * 2
        + [dma((4,))]
        + [dma((3, parts, groups))] * 2
        + [dma((parts, groups))] * 4
        + [dma((3, parts))],
        compiler_params=pltpu.CompilerParams(
            collective_id=0, has_side_effects=True, vmem_limit_bytes=52 * 1024 * 1024
        ),
    )(coef, high, low, f, x, dy, gate)


def shards(inputs, gate, grad_out, filters):
    groups = lax.axis_size("ctx")
    channels, width = inputs.shape[1:]
    owned = channels // groups

    def blocks(array):
        return array.reshape(groups, owned, width)

    gf, gi, gg = fused(*(blocks(v) for v in (filters, inputs, grad_out, gate)))
    return (
        gi.reshape(1, channels, width),
        gg.reshape(1, channels, width),
        gf.reshape(channels, width),
    )


def solution(mesh):
    placed = (P("dp", "tp", "ctx"), P("dp", "tp", "ctx"), P("dp", "tp", "ctx"), P("tp", "ctx"))
    return jax.shard_map(
        shards,
        mesh=mesh,
        in_specs=placed,
        out_specs=(P("dp", "tp", "ctx"), P("dp", "tp", "ctx"), P("tp", "ctx")),
        check_vma=False,
    )
```

```python
import math
from functools import partial

import jax
import jax.numpy as jnp
import numpy as np
from jax import lax
from jax.experimental import pallas as pl
from jax.experimental.pallas import tpu as pltpu
from jax.sharding import PartitionSpec as P

BF16 = jnp.bfloat16
F32 = jnp.float32
PARTS = 2
MESH = pl.DeviceIdType.MESH


def tables(groups, width):
    outer = 2 * groups
    total = outer * width
    freqs = groups + 1
    k1 = np.arange(freqs)[:, None, None]
    b = np.arange(width)[None, :, None]
    k2 = np.arange(width)[None, None, :]
    angle = 2.0 * math.pi * ((b * (k1 + outer * k2)) % total) / total
    cosine, sine = np.cos(angle), -np.sin(angle)
    top = np.concatenate([cosine, sine], axis=2)
    bottom = np.concatenate([-sine, cosine], axis=2)
    matrix = np.concatenate([top, bottom], axis=1).astype(np.float32)
    high = matrix.astype(BF16)
    low = (matrix - high.astype(np.float32)).astype(BF16)
    phase = 2.0 * math.pi * ((np.arange(freqs)[:, None] * np.arange(groups)[None, :]) % outer) / outer
    weight = np.full((freqs, 1), 2.0)
    weight[0] = weight[-1] = 1.0
    weight = weight / total
    coef = np.stack([np.cos(phase), -np.sin(phase), weight * np.cos(phase), -weight * np.sin(phase)], axis=1)
    return high, low, coef.reshape(freqs * 4, groups).astype(np.float32)


def split(value):
    high = value.astype(BF16)
    return high, (value - high.astype(F32)).astype(BF16)


def greet(me, groups, twin):
    barrier = pltpu.get_barrier_semaphore()

    def hail(o, _):
        pl.semaphore_signal(barrier, inc=1, device_id={"ctx": lax.rem(me + o, groups)}, device_id_type=MESH)
        return 0

    lax.fori_loop(1, groups, hail, 0)
    pl.semaphore_signal(barrier, inc=1, device_id={"dp": twin}, device_id_type=MESH)
    pl.semaphore_wait(barrier, groups)


def fused_kernel(groups, parts, coef, high_ref, low_ref, f_ref, x_ref, dy_ref, gate_ref, ogf_ref, ogi_ref, ogg_ref, *scratch):
    (filt, recv_sig, sig, a_hi, a_lo, spec, acc, gf, gi, gg, inbox, total) = scratch[:12]
    (f_send, f_recv, f_pass_send, f_pass_recv, x_send, x_recv, keep_sem) = scratch[12:19]
    (o_send, o_recv, twin_send, twin_recv, pass_send, pass_recv, out_sem) = scratch[19:26]
    mh_ref, ml_ref, table_sem = scratch[26:]
    owned, width = f_ref.shape[1:]
    chunk = owned // parts
    half, slim = owned // 2, chunk // 2
    rows = min(32, chunk)
    pieces = chunk // rows
    me, dp = lax.axis_index("ctx"), lax.axis_index("dp")
    twin = 1 - dp
    sources = (x_ref, dy_ref, gate_ref)

    def f_rows(which):
        return pl.ds(pl.multiple_of(which * half, half), half)

    def part(q):
        return pl.ds(q * chunk, chunk)

    def slim_rows(q, which):
        return pl.ds(pl.multiple_of(q * chunk + which * slim, slim), slim)

    def remote(source, target, send, recv, device):
        return pltpu.make_async_remote_copy(
            src_ref=source, dst_ref=target, send_sem=send, recv_sem=recv, device_id=device, device_id_type=MESH
        )

    def f_push(peer, slot):
        return remote(
            f_ref.at[peer, f_rows(dp)], filt.at[slot, f_rows(dp)], f_send.at[peer], f_recv.at[slot], {"ctx": peer}
        )

    def f_hand(slot, which):
        block = filt.at[slot, f_rows(which)]
        return remote(block, block, f_pass_send.at[slot], f_pass_recv.at[slot], {"dp": twin})

    def x_push(s, q, peer, slot):
        return remote(
            sources[s].at[peer, part(q)],
            recv_sig.at[s, slot, part(q)],
            x_send.at[s, q, peer],
            x_recv.at[s, q, slot],
            {"ctx": peer},
        )

    def keep(s):
        if s == 3:
            return pltpu.make_async_copy(f_ref.at[me], filt.at[me], keep_sem.at[3])
        return pltpu.make_async_copy(sources[s].at[me], recv_sig.at[s, me], keep_sem.at[s])

    def trade(q, a):
        return remote(
            gf.at[a, slim_rows(q, twin)], inbox.at[q, a], twin_send.at[q, a], twin_recv.at[q, a], {"dp": twin}
        )

    def out_push(s, q, peer, slot):
        if s == 0:
            source, target = total.at[q, peer], ogf_ref.at[slot, slim_rows(q, dp)]
        else:
            source, target = (gi, gg)[s - 1].at[peer, part(q)], (ogi_ref, ogg_ref)[s - 1].at[slot, part(q)]
        return remote(source, target, o_send.at[s, q, peer], o_recv.at[s, q, slot], {"ctx": peer})

    def out_keep(s, q):
        if s == 0:
            return pltpu.make_async_copy(total.at[q, me], ogf_ref.at[me, slim_rows(q, dp)], out_sem.at[0, q])
        source, target = (gi, gg)[s - 1].at[me, part(q)], (ogi_ref, ogg_ref)[s - 1].at[me, part(q)]
        return pltpu.make_async_copy(source, target, out_sem.at[s, q])

    def hand(source, q, slot, which):
        return remote(
            source, ogf_ref.at[slot, slim_rows(q, which)], pass_send.at[q, slot], pass_recv.at[q, slot], {"dp": twin}
        )

    def each(first, body, last=groups):
        def run(o, _):
            body(lax.rem(me + o, groups), lax.rem(me + groups - o, groups))
            return 0

        lax.fori_loop(first, last, run, 0)

    def load_tables():
        return (
            pltpu.make_async_copy(high_ref, mh_ref, table_sem.at[0]),
            pltpu.make_async_copy(low_ref, ml_ref, table_sem.at[1]),
        )

    def compute(q, midway):
        def by_rows(body):
            def run(r, _):
                body(pl.multiple_of(r * rows, rows))
                return 0

            lax.fori_loop(0, pieces, run, 0)

        def fill(at):
            near, far = pl.ds(at, rows), pl.ds(pl.multiple_of(at + q * chunk, rows), rows)
            for a in range(groups):
                sig[0, a, near, :] = recv_sig[0, a, far, :].astype(F32)
                sig[1, a, near, :] = recv_sig[1, a, far, :].astype(F32) * recv_sig[2, a, far, :].astype(F32)
                sig[2, a, near, :] = filt[a, far, :]
                for s in range(3):
                    acc[s, a, near, :] = jnp.zeros((rows, width), F32)

        by_rows(fill)

        def frequency(k, _):
            base = k * 4

            def put(s, at, real, imag):
                to = pl.ds(pl.multiple_of(at + s * chunk, rows), rows)
                a_hi[to, :width], a_lo[to, :width] = split(real)
                a_hi[to, width:], a_lo[to, width:] = split(imag)

            def take(s, at):
                to = pl.ds(pl.multiple_of(at + s * chunk, rows), rows)
                return spec[to, :width], spec[to, width:]

            def forward(at):
                for s in range(3):
                    real = imag = None
                    for a in range(groups):
                        value = sig[s, a, pl.ds(at, rows), :]
                        re, im = value * coef[base, a], value * coef[base + 1, a]
                        real = re if real is None else real + re
                        imag = im if imag is None else imag + im
                    put(s, at, real, imag)

            def multiply(contract):
                dims = (((1,), (contract,)), ((), ()))
                dot = partial(lax.dot_general, dimension_numbers=dims, preferred_element_type=F32)
                high, low = a_hi[...], a_lo[...]
                spec[...] = dot(high, mh_ref[k]) + dot(low, mh_ref[k]) + dot(high, ml_ref[k])

            def pointwise(at):
                (xr, xi), (pr, pi), (fr, fi) = take(0, at), take(1, at), take(2, at)
                put(0, at, fr * xr - fi * xi, fr * xi + fi * xr)
                put(1, at, fr * pr + fi * pi, fr * pi - fi * pr)
                put(2, at, xr * pr + xi * pi, xr * pi - xi * pr)

            def inverse(at):
                for s in range(3):
                    real, imag = take(s, at)
                    for a in range(groups):
                        acc[s, a, pl.ds(at, rows), :] += real * coef[base + 2, a] + imag * coef[base + 3, a]

            by_rows(forward)
            multiply(0)
            by_rows(pointwise)
            multiply(1)
            by_rows(inverse)
            return 0

        middle = (groups + 1) // 2 + 1
        lax.fori_loop(0, middle, frequency, 0)
        midway()
        lax.fori_loop(middle, groups + 1, frequency, 0)

        def finish(at):
            near, far = pl.ds(at, rows), pl.ds(pl.multiple_of(at + q * chunk, rows), rows)
            for a in range(groups):
                gg[a, far, :] = (recv_sig[1, a, far, :].astype(F32) * acc[0, a, near, :]).astype(BF16)
                gi[a, far, :] = acc[1, a, near, :].astype(BF16)
                gf[a, far, :] = acc[2, a, near, :]

        by_rows(finish)

    def combine(q):
        def add(a):
            trade(q, a).wait_recv()
            total[q, a] = gf[a, slim_rows(q, dp), :] + inbox[q, a]

        def reduce(to, origin):
            add(to)
            out_push(0, q, to, me).start()

        each(1, reduce)
        add(me)
        out_keep(0, q).start()
        hand(total.at[q, me], q, me, dp).start()

    greet(me, groups, twin)
    each(1, lambda to, origin: f_push(to, me).start())
    for q in range(parts):
        for s in range(3):
            each(1, lambda to, origin, s=s, q=q: x_push(s, q, to, me).start())
    for copy in (*load_tables(), *(keep(s) for s in range(4))):
        copy.start()

    def f_relay(to, origin):
        f_push(origin, origin).wait_recv()
        f_hand(origin, dp).start()

    each(1, f_relay)

    def f_settle(to, origin):
        f_hand(origin, dp).wait_send()
        f_hand(origin, twin).wait_recv()
        f_push(origin, origin).wait_send()

    each(1, f_settle)
    for copy in (*load_tables(), *(keep(s) for s in range(4))):
        copy.wait()
    for q in range(parts):
        for s in range(3):
            each(1, lambda to, origin, s=s, q=q: x_push(s, q, origin, origin).wait_recv())
        compute(q, partial(combine, q - 1) if q else lambda: None)
        each(1, lambda to, origin, q=q: trade(q, to).start(), groups + 1)
        for s in (1, 2):
            each(1, lambda to, origin, s=s, q=q: out_push(s, q, to, me).start())
            out_keep(s, q).start()

    combine(parts - 1)
    for q in range(parts):

        def relay(to, origin, q=q):
            out_push(0, q, origin, origin).wait_recv()
            hand(ogf_ref.at[origin, slim_rows(q, dp)], q, origin, dp).start()

        each(1, relay)
    for q in range(parts):

        def settle(a, origin, q=q):
            trade(q, a).wait_send()
            hand(total.at[q, me], q, a, dp).wait_send()
            hand(total.at[q, me], q, a, twin).wait_recv()

        each(1, settle, groups + 1)
        for s in range(3):

            def done(to, origin, q=q, s=s):
                x_push(s, q, origin, origin).wait_send()
                if s:
                    out_push(s, q, origin, origin).wait_recv()
                out_push(s, q, origin, origin).wait_send()

            each(1, done)
            out_keep(s, q).wait()


def fused(f, x, dy, gate):
    groups, owned, width = f.shape
    parts = PARTS if owned % (16 * PARTS) == 0 else 1
    chunk = owned // parts
    high, low, coef = tables(groups, width)
    anywhere = pl.BlockSpec(memory_space=pl.ANY)
    dma = pltpu.SemaphoreType.DMA
    shape = (groups, owned, width)
    slim = (parts, groups, chunk // 2, width)
    return pl.pallas_call(
        partial(fused_kernel, groups, parts),
        in_specs=[pl.BlockSpec(memory_space=pltpu.SMEM)] + [anywhere] * 6,
        out_specs=[anywhere] * 3,
        out_shape=[
            jax.ShapeDtypeStruct(shape, F32),
            jax.ShapeDtypeStruct(shape, BF16),
            jax.ShapeDtypeStruct(shape, BF16),
        ],
        scratch_shapes=[
            pltpu.VMEM(shape, F32),
            pltpu.VMEM((3,) + shape, BF16),
            pltpu.VMEM((3, groups, chunk, width), F32),
            pltpu.VMEM((3 * chunk, 2 * width), BF16),
            pltpu.VMEM((3 * chunk, 2 * width), BF16),
            pltpu.VMEM((3 * chunk, 2 * width), F32),
            pltpu.VMEM((3, groups, chunk, width), F32),
            pltpu.VMEM(shape, F32),
            pltpu.VMEM(shape, BF16),
            pltpu.VMEM(shape, BF16),
            pltpu.VMEM(slim, F32),
            pltpu.VMEM(slim, F32),
        ]
        + [dma((groups,))] * 4
        + [dma((3, parts, groups))] * 2
        + [dma((4,))]
        + [dma((3, parts, groups))] * 2
        + [dma((parts, groups))] * 4
        + [dma((3, parts))]
        + [pltpu.VMEM(high.shape, BF16)] * 2
        + [dma((2,))],
        compiler_params=pltpu.CompilerParams(
            collective_id=0, has_side_effects=True, vmem_limit_bytes=52 * 1024 * 1024
        ),
    )(coef, high, low, f, x, dy, gate)


def shards(inputs, gate, grad_out, filters):
    groups = lax.axis_size("ctx")
    channels, width = inputs.shape[1:]
    owned = channels // groups

    def blocks(array):
        return array.reshape(groups, owned, width)

    gf, gi, gg = fused(*(blocks(v) for v in (filters, inputs, grad_out, gate)))
    return (
        gi.reshape(1, channels, width),
        gg.reshape(1, channels, width),
        gf.reshape(channels, width),
    )


def solution(mesh):
    placed = (P("dp", "tp", "ctx"), P("dp", "tp", "ctx"), P("dp", "tp", "ctx"), P("tp", "ctx"))
    return jax.shard_map(
        shards,
        mesh=mesh,
        in_specs=placed,
        out_specs=(P("dp", "tp", "ctx"), P("dp", "tp", "ctx"), P("tp", "ctx")),
        check_vma=False,
    )
```

```python
import math
from functools import partial

import jax
import jax.numpy as jnp
import numpy as np
from jax import lax
from jax.experimental import pallas as pl
from jax.experimental.pallas import tpu as pltpu
from jax.sharding import PartitionSpec as P

BF16 = jnp.bfloat16
F32 = jnp.float32
PARTS = 4
MESH = pl.DeviceIdType.MESH


def tables(groups, width):
    outer = 2 * groups
    total = outer * width
    freqs = groups + 1
    k1 = np.arange(freqs)[:, None, None]
    b = np.arange(width)[None, :, None]
    k2 = np.arange(width)[None, None, :]
    angle = 2.0 * math.pi * ((b * (k1 + outer * k2)) % total) / total
    cosine, sine = np.cos(angle), -np.sin(angle)
    top = np.concatenate([cosine, sine], axis=2)
    bottom = np.concatenate([-sine, cosine], axis=2)
    matrix = np.concatenate([top, bottom], axis=1).astype(np.float32)
    high = matrix.astype(BF16)
    low = (matrix - high.astype(np.float32)).astype(BF16)
    phase = 2.0 * math.pi * ((np.arange(freqs)[:, None] * np.arange(groups)[None, :]) % outer) / outer
    weight = np.full((freqs, 1), 2.0)
    weight[0] = weight[-1] = 1.0
    weight = weight / total
    coef = np.stack([np.cos(phase), -np.sin(phase), weight * np.cos(phase), -weight * np.sin(phase)], axis=1)
    return high, low, coef.reshape(freqs * 4, groups).astype(np.float32)


def split(value):
    high = value.astype(BF16)
    return high, (value - high.astype(F32)).astype(BF16)


def greet(me, groups, twin):
    barrier = pltpu.get_barrier_semaphore()

    def hail(o, _):
        pl.semaphore_signal(barrier, inc=1, device_id={"ctx": lax.rem(me + o, groups)}, device_id_type=MESH)
        return 0

    lax.fori_loop(1, groups, hail, 0)
    pl.semaphore_signal(barrier, inc=1, device_id={"dp": twin}, device_id_type=MESH)
    pl.semaphore_wait(barrier, groups)


def fused_kernel(groups, parts, coef, high_ref, low_ref, f_ref, x_ref, dy_ref, gate_ref, ogf_ref, ogi_ref, ogg_ref, *scratch):
    (filt, recv_sig, sig, a_hi, a_lo, spec, acc, gf, gi, gg, inbox, total) = scratch[:12]
    (f_send, f_recv, f_pass_send, f_pass_recv, x_send, x_recv, keep_sem) = scratch[12:19]
    (o_send, o_recv, twin_send, twin_recv, pass_send, pass_recv, out_sem) = scratch[19:26]
    mh_ref, ml_ref, table_sem = scratch[26:]
    owned, width = f_ref.shape[1:]
    chunk = owned // parts
    half, slim = owned // 2, chunk // 2
    rows = min(32, chunk)
    pieces = chunk // rows
    me, dp = lax.axis_index("ctx"), lax.axis_index("dp")
    twin = 1 - dp
    sources = (x_ref, dy_ref, gate_ref)

    def f_rows(which):
        return pl.ds(pl.multiple_of(which * half, half), half)

    def part(q):
        return pl.ds(q * chunk, chunk)

    def slim_rows(q, which):
        return pl.ds(pl.multiple_of(q * chunk + which * slim, slim), slim)

    def remote(source, target, send, recv, device):
        return pltpu.make_async_remote_copy(
            src_ref=source, dst_ref=target, send_sem=send, recv_sem=recv, device_id=device, device_id_type=MESH
        )

    def f_push(peer, slot):
        return remote(
            f_ref.at[peer, f_rows(dp)], filt.at[slot, f_rows(dp)], f_send.at[peer], f_recv.at[slot], {"ctx": peer}
        )

    def f_hand(slot, which):
        block = filt.at[slot, f_rows(which)]
        return remote(block, block, f_pass_send.at[slot], f_pass_recv.at[slot], {"dp": twin})

    def x_push(s, q, peer, slot):
        return remote(
            sources[s].at[peer, part(q)],
            recv_sig.at[s, slot, part(q)],
            x_send.at[s, q, peer],
            x_recv.at[s, q, slot],
            {"ctx": peer},
        )

    def keep(s):
        if s == 3:
            return pltpu.make_async_copy(f_ref.at[me], filt.at[me], keep_sem.at[3])
        return pltpu.make_async_copy(sources[s].at[me], recv_sig.at[s, me], keep_sem.at[s])

    def trade(q, a):
        return remote(
            gf.at[a, slim_rows(q, twin)], inbox.at[q, a], twin_send.at[q, a], twin_recv.at[q, a], {"dp": twin}
        )

    def out_push(s, q, peer, slot):
        if s == 0:
            source, target = total.at[q, peer], ogf_ref.at[slot, slim_rows(q, dp)]
        else:
            source, target = (gi, gg)[s - 1].at[peer, part(q)], (ogi_ref, ogg_ref)[s - 1].at[slot, part(q)]
        return remote(source, target, o_send.at[s, q, peer], o_recv.at[s, q, slot], {"ctx": peer})

    def out_keep(s, q):
        if s == 0:
            return pltpu.make_async_copy(total.at[q, me], ogf_ref.at[me, slim_rows(q, dp)], out_sem.at[0, q])
        source, target = (gi, gg)[s - 1].at[me, part(q)], (ogi_ref, ogg_ref)[s - 1].at[me, part(q)]
        return pltpu.make_async_copy(source, target, out_sem.at[s, q])

    def hand(source, q, slot, which):
        return remote(
            source, ogf_ref.at[slot, slim_rows(q, which)], pass_send.at[q, slot], pass_recv.at[q, slot], {"dp": twin}
        )

    def each(first, body, last=groups):
        def run(o, _):
            body(lax.rem(me + o, groups), lax.rem(me + groups - o, groups))
            return 0

        lax.fori_loop(first, last, run, 0)

    def load_tables():
        return (
            pltpu.make_async_copy(high_ref, mh_ref, table_sem.at[0]),
            pltpu.make_async_copy(low_ref, ml_ref, table_sem.at[1]),
        )

    def compute(q, midway):
        def by_rows(body):
            def run(r, _):
                body(pl.multiple_of(r * rows, rows))
                return 0

            lax.fori_loop(0, pieces, run, 0)

        def fill(at):
            near, far = pl.ds(at, rows), pl.ds(pl.multiple_of(at + q * chunk, rows), rows)
            for a in range(groups):
                sig[0, a, near, :] = recv_sig[0, a, far, :].astype(F32)
                sig[1, a, near, :] = recv_sig[1, a, far, :].astype(F32) * recv_sig[2, a, far, :].astype(F32)
                sig[2, a, near, :] = filt[a, far, :]
                for s in range(3):
                    acc[s, a, near, :] = jnp.zeros((rows, width), F32)

        by_rows(fill)

        def frequency(k, _):
            base = k * 4

            def put(s, at, real, imag):
                to = pl.ds(pl.multiple_of(at + s * chunk, rows), rows)
                a_hi[to, :width], a_lo[to, :width] = split(real)
                a_hi[to, width:], a_lo[to, width:] = split(imag)

            def take(s, at):
                to = pl.ds(pl.multiple_of(at + s * chunk, rows), rows)
                return spec[to, :width], spec[to, width:]

            def forward(at):
                for s in range(3):
                    real = imag = None
                    for a in range(groups):
                        value = sig[s, a, pl.ds(at, rows), :]
                        re, im = value * coef[base, a], value * coef[base + 1, a]
                        real = re if real is None else real + re
                        imag = im if imag is None else imag + im
                    put(s, at, real, imag)

            def multiply(contract):
                dims = (((1,), (contract,)), ((), ()))
                dot = partial(lax.dot_general, dimension_numbers=dims, preferred_element_type=F32)
                high, low = a_hi[...], a_lo[...]
                spec[...] = dot(high, mh_ref[k]) + dot(low, mh_ref[k]) + dot(high, ml_ref[k])

            def pointwise(at):
                (xr, xi), (pr, pi), (fr, fi) = take(0, at), take(1, at), take(2, at)
                put(0, at, fr * xr - fi * xi, fr * xi + fi * xr)
                put(1, at, fr * pr + fi * pi, fr * pi - fi * pr)
                put(2, at, xr * pr + xi * pi, xr * pi - xi * pr)

            def inverse(at):
                for s in range(3):
                    real, imag = take(s, at)
                    for a in range(groups):
                        acc[s, a, pl.ds(at, rows), :] += real * coef[base + 2, a] + imag * coef[base + 3, a]

            by_rows(forward)
            multiply(0)
            by_rows(pointwise)
            multiply(1)
            by_rows(inverse)
            return 0

        middle = (groups + 1) // 2 + 1
        lax.fori_loop(0, middle, frequency, 0)
        midway()
        lax.fori_loop(middle, groups + 1, frequency, 0)

        def finish(at):
            near, far = pl.ds(at, rows), pl.ds(pl.multiple_of(at + q * chunk, rows), rows)
            for a in range(groups):
                gg[a, far, :] = (recv_sig[1, a, far, :].astype(F32) * acc[0, a, near, :]).astype(BF16)
                gi[a, far, :] = acc[1, a, near, :].astype(BF16)
                gf[a, far, :] = acc[2, a, near, :]

        by_rows(finish)

    def combine(q):
        def add(a):
            trade(q, a).wait_recv()
            total[q, a] = gf[a, slim_rows(q, dp), :] + inbox[q, a]

        def reduce(to, origin):
            add(to)
            out_push(0, q, to, me).start()

        each(1, reduce)
        add(me)
        out_keep(0, q).start()
        hand(total.at[q, me], q, me, dp).start()

    greet(me, groups, twin)
    each(1, lambda to, origin: f_push(to, me).start())
    for q in range(parts):
        for s in range(3):
            each(1, lambda to, origin, s=s, q=q: x_push(s, q, to, me).start())
    for copy in (*load_tables(), *(keep(s) for s in range(4))):
        copy.start()

    def f_relay(to, origin):
        f_push(origin, origin).wait_recv()
        f_hand(origin, dp).start()

    each(1, f_relay)

    def f_settle(to, origin):
        f_hand(origin, dp).wait_send()
        f_hand(origin, twin).wait_recv()
        f_push(origin, origin).wait_send()

    each(1, f_settle)
    for copy in (*load_tables(), *(keep(s) for s in range(4))):
        copy.wait()
    for q in range(parts):
        for s in range(3):
            each(1, lambda to, origin, s=s, q=q: x_push(s, q, origin, origin).wait_recv())
        compute(q, partial(combine, q - 1) if q else lambda: None)
        each(1, lambda to, origin, q=q: trade(q, to).start(), groups + 1)
        for s in (1, 2):
            each(1, lambda to, origin, s=s, q=q: out_push(s, q, to, me).start())
            out_keep(s, q).start()

    combine(parts - 1)
    for q in range(parts):

        def relay(to, origin, q=q):
            out_push(0, q, origin, origin).wait_recv()
            hand(ogf_ref.at[origin, slim_rows(q, dp)], q, origin, dp).start()

        each(1, relay)
    for q in range(parts):

        def settle(a, origin, q=q):
            trade(q, a).wait_send()
            hand(total.at[q, me], q, a, dp).wait_send()
            hand(total.at[q, me], q, a, twin).wait_recv()

        each(1, settle, groups + 1)
        for s in range(3):

            def done(to, origin, q=q, s=s):
                x_push(s, q, origin, origin).wait_send()
                if s:
                    out_push(s, q, origin, origin).wait_recv()
                out_push(s, q, origin, origin).wait_send()

            each(1, done)
            out_keep(s, q).wait()


def fused(f, x, dy, gate):
    groups, owned, width = f.shape
    parts = PARTS if owned % (16 * PARTS) == 0 else 1
    chunk = owned // parts
    high, low, coef = tables(groups, width)
    anywhere = pl.BlockSpec(memory_space=pl.ANY)
    dma = pltpu.SemaphoreType.DMA
    shape = (groups, owned, width)
    slim = (parts, groups, chunk // 2, width)
    return pl.pallas_call(
        partial(fused_kernel, groups, parts),
        in_specs=[pl.BlockSpec(memory_space=pltpu.SMEM)] + [anywhere] * 6,
        out_specs=[anywhere] * 3,
        out_shape=[
            jax.ShapeDtypeStruct(shape, F32),
            jax.ShapeDtypeStruct(shape, BF16),
            jax.ShapeDtypeStruct(shape, BF16),
        ],
        scratch_shapes=[
            pltpu.VMEM(shape, F32),
            pltpu.VMEM((3,) + shape, BF16),
            pltpu.VMEM((3, groups, chunk, width), F32),
            pltpu.VMEM((3 * chunk, 2 * width), BF16),
            pltpu.VMEM((3 * chunk, 2 * width), BF16),
            pltpu.VMEM((3 * chunk, 2 * width), F32),
            pltpu.VMEM((3, groups, chunk, width), F32),
            pltpu.VMEM(shape, F32),
            pltpu.VMEM(shape, BF16),
            pltpu.VMEM(shape, BF16),
            pltpu.VMEM(slim, F32),
            pltpu.VMEM(slim, F32),
        ]
        + [dma((groups,))] * 4
        + [dma((3, parts, groups))] * 2
        + [dma((4,))]
        + [dma((3, parts, groups))] * 2
        + [dma((parts, groups))] * 4
        + [dma((3, parts))]
        + [pltpu.VMEM(high.shape, BF16)] * 2
        + [dma((2,))],
        compiler_params=pltpu.CompilerParams(
            collective_id=0, has_side_effects=True, vmem_limit_bytes=52 * 1024 * 1024
        ),
    )(coef, high, low, f, x, dy, gate)


def shards(inputs, gate, grad_out, filters):
    groups = lax.axis_size("ctx")
    channels, width = inputs.shape[1:]
    owned = channels // groups

    def blocks(array):
        return array.reshape(groups, owned, width)

    gf, gi, gg = fused(*(blocks(v) for v in (filters, inputs, grad_out, gate)))
    return (
        gi.reshape(1, channels, width),
        gg.reshape(1, channels, width),
        gf.reshape(channels, width),
    )


def solution(mesh):
    placed = (P("dp", "tp", "ctx"), P("dp", "tp", "ctx"), P("dp", "tp", "ctx"), P("tp", "ctx"))
    return jax.shard_map(
        shards,
        mesh=mesh,
        in_specs=placed,
        out_specs=(P("dp", "tp", "ctx"), P("dp", "tp", "ctx"), P("tp", "ctx")),
        check_vma=False,
    )
```
